32 devices in a mesh: dp: 32 (over z, y, x, core).
Axes of the slice: x: 2, y: 2, z: 4, core: 2. Of those that a mesh axis runs over, the one named last changes fastest.
Arguments:
- hidden_in: bfloat16 [128, 128, 768], P('dp'), may hold values from -6 to 6
- attention_keep: int32 [2, 128, 128, 768], P(None, 'dp'), may hold values 0 or 1
- feedforward_keep: int32 [2, 128, 128, 768], P(None, 'dp'), may hold values 0 or 1
- lengths: int32 [128], P('dp'), may hold values from 5 to 128, as said below
- cotangent: bfloat16 [2, 128, 128, 768], P(None, 'dp'), may hold values from -6 to 6
- query_weight: bfloat16 [768, 768], P('dp'), may hold values from -0.21875 to 0.21875
- key_weight: bfloat16 [768, 768], P('dp'), may hold values from -0.21875 to 0.21875
- value_weight: bfloat16 [768, 768], P('dp'), may hold values from -0.21875 to 0.21875
- output_weight: bfloat16 [768, 768], P('dp'), may hold values from -1.75 to 1.75
- inner_weight: bfloat16 [768, 3072], P('dp'), may hold values from -0.21875 to 0.21875
- outer_weight: bfloat16 [3072, 768], P('dp'), may hold values from -0.15625 to 0.15625
- pooler_weight: bfloat16 [768, 768], P('dp'), may hold values from -0.4375 to 0.4375
- query_bias: bfloat16 [768], P('dp'), may hold values from -3 to 3
- value_bias: bfloat16 [768], P('dp'), may hold values from -3 to 3
- output_bias: bfloat16 [768], P('dp'), may hold values from -3 to 3
- first_gain: bfloat16 [768], P('dp'), may hold values from 0.5 to 1.5
- first_shift: bfloat16 [768], P('dp'), may hold values from -3 to 3
- inner_bias: bfloat16 [3072], P('dp'), may hold values from -3 to 3
- outer_bias: bfloat16 [768], P('dp'), may hold values from -3 to 3
- second_gain: bfloat16 [768], P('dp'), may hold values from 0.5 to 1.5
- second_shift: bfloat16 [768], P('dp'), may hold values from -3 to 3
- pooler_bias: bfloat16 [768], P('dp'), may hold values from -3 to 3
Outputs:
- loss_value: float32 [], replicated
- hidden_out: bfloat16 [2, 128, 128, 768], P(None, 'dp')
- hidden_grad: float32 [128, 128, 768], P('dp')
- query_weight_grad: float32 [768, 768], P('dp')
- key_weight_grad: float32 [768, 768], P('dp')
- value_weight_grad: float32 [768, 768], P('dp')
- output_weight_grad: float32 [768, 768], P('dp')
- inner_weight_grad: float32 [768, 3072], P('dp')
- outer_weight_grad: float32 [3072, 768], P('dp')
- pooler_weight_grad: float32 [768, 768], P('dp')
- query_bias_grad: float32 [768], P('dp')
- value_bias_grad: float32 [768], P('dp')
- output_bias_grad: float32 [768], P('dp')
- first_gain_grad: float32 [768], P('dp')
- first_shift_grad: float32 [768], P('dp')
- inner_bias_grad: float32 [3072], P('dp')
- outer_bias_grad: float32 [768], P('dp')
- second_gain_grad: float32 [768], P('dp')
- second_shift_grad: float32 [768], P('dp')
- pooler_bias_grad: float32 [768], P('dp')
The draws below stay inside these ranges and needn't reach their ends.
Inputs may be any that keep to these rules, and one draw needn't show every extreme that they name: `lengths`: a sentence's real tokens fill its first slots; some sentence has 128.
All inputs are finite; a program needn't handle non-finite values. No bound on the sum of `attention_keep` or of `feedforward_keep` on one device may be relied on, other than what follows from the above.
Results may differ from the reference program's by a relative error of at most 0.014.
Values may be sent and summed in bfloat16 or wider, within the bound.
No kernel may reach another device: no remote copies, remote signals or barrier semaphores. Data moves between devices by JAX's collectives and lax.ppermute only.
A program may use at most 192 MiB of HBM per device.

```python
import math
import jax
import jax.numpy as jnp
from jax import lax

D = 768
HD = 64
FF = 3072
LEN = 128
SENT_DEV = 4
SENTS = 128


def draw_lengths(key, part):
    spread = LEN - 5
    left = jax.random.randint(jax.random.fold_in(key, 11), (SENTS,), 0, spread + 1)
    right = jax.random.randint(jax.random.fold_in(key, 12), (SENTS,), 0, spread + 1)
    drawn = LEN - left * right // spread
    chosen = jax.random.randint(jax.random.fold_in(key, 13), (), 0, SENTS)
    return jnp.where(jnp.arange(SENTS) == chosen, LEN, drawn).astype(jnp.int32)


def touch_ends(values, rng, least, top_value):
    index_at = [jax.random.randint(jax.random.fold_in(rng, axis), (), 0, length) for axis, length in enumerate(values.shape)]
    widest = values.shape.index(max(values.shape))
    neighbour = index_at[:widest] + [(index_at[widest] + 1) % values.shape[widest]] + index_at[widest + 1:]
    return values.at[tuple(index_at)].set(least).at[tuple(neighbour)].set(top_value)


def levels(rng, shape, split, low, largest):
    def one(dim, shards_of):
        steps = jax.random.uniform(jax.random.fold_in(jax.random.fold_in(rng, 6), dim), (shards_of,), jnp.float32, low / len(split), largest / len(split))
        return jnp.repeat(jnp.exp(steps), shape[dim] // shards_of).reshape((-1,) + (1,) * (len(shape) - dim - 1))

    loudness = one(*split[0])
    for cut in split[1:]:
        loudness = loudness * one(*cut)
    return loudness


def scatter_about(stream_key, extent, scale, reach, shards=(), held_as=jnp.bfloat16):
    values = jax.random.normal(stream_key, extent, jnp.float32) * scale
    if len(shards) > 0:
        values = levels(stream_key, extent, shards, -0.22, 0.18) * values
    return jnp.clip(values, min=-reach, max=reach).astype(held_as)


def setup_inputs(seed: int = 0) -> dict:
    key_list = jax.random.split(jax.random.key(seed), 23)
    return {
        "hidden_in": scatter_about(key_list[0], (SENTS, LEN, D), 1.0, 6.0, ((0, 32),)),
        "attention_keep": touch_ends((jax.random.randint(key_list[1], (2, SENTS, LEN, D), 0, 10) < 9).astype(jnp.int32), jax.random.fold_in(key_list[1], 1), 0, 1),
        "feedforward_keep": touch_ends((jax.random.randint(key_list[2], (2, SENTS, LEN, D), 0, 10) < 9).astype(jnp.int32), jax.random.fold_in(key_list[2], 1), 0, 1),
        "lengths": draw_lengths(jax.random.fold_in(key_list[22], 71), 0),
        "cotangent": scatter_about(key_list[4], (2, SENTS, LEN, D), 1.0, 6.0, ((1, 32),)),
        "query_weight": scatter_about(key_list[5], (D, D), D ** -0.5, 0.21875, ((0, 32),)),
        "key_weight": scatter_about(key_list[6], (D, D), D ** -0.5, 0.21875, ((0, 32),)),
        "value_weight": scatter_about(key_list[7], (D, D), D ** -0.5, 0.21875, ((0, 32),)),
        "output_weight": scatter_about(key_list[8], (D, D), (D // 64) ** -0.5, 1.75, ((0, 32),)),
        "inner_weight": scatter_about(key_list[9], (D, FF), D ** -0.5, 0.21875, ((0, 32),)),
        "outer_weight": scatter_about(key_list[10], (FF, D), (FF // 2) ** -0.5, 0.15625, ((0, 32),)),
        "pooler_weight": scatter_about(key_list[11], (D, D), (D // 4) ** -0.5, 0.4375, ((0, 32),)),
        "query_bias": scatter_about(key_list[12], (D,), 0.5, 3.0, ((0, 32),)),
        "value_bias": scatter_about(key_list[13], (D,), 0.5, 3.0, ((0, 32),)),
        "output_bias": scatter_about(key_list[14], (D,), 0.5, 3.0, ((0, 32),)),
        "first_gain": jnp.clip(1.0 + 0.1 * jax.random.normal(key_list[15], (D,), jnp.float32), 0.5, 1.5).astype(jnp.bfloat16),
        "first_shift": scatter_about(key_list[16], (D,), 0.5, 3.0, ((0, 32),)),
        "inner_bias": scatter_about(key_list[17], (FF,), 0.5, 3.0, ((0, 32),)),
        "outer_bias": scatter_about(key_list[18], (D,), 0.5, 3.0, ((0, 32),)),
        "second_gain": jnp.clip(1.0 + 0.1 * jax.random.normal(key_list[19], (D,), jnp.float32), 0.5, 1.5).astype(jnp.bfloat16),
        "second_shift": scatter_about(key_list[20], (D,), 0.5, 3.0, ((0, 32),)),
        "pooler_bias": scatter_about(key_list[21], (D,), 0.5, 3.0, ((0, 32),)),
    }


@jax.custom_vjp
def low(v):
    return lax.optimization_barrier(v.astype(jnp.bfloat16)).astype(jnp.float32)

@jax.custom_vjp
def low_back(v):
    return v

def low_keep(v):
    return (low(v), None)

def low_pass(kept, grad):
    return (grad,)

def back_keep(v):
    return (v, None)

def back_low(kept, grad):
    return (low(grad),)
low.defvjp(low_keep, low_pass)
low_back.defvjp(back_keep, back_low)
highest = lax.Precision.HIGHEST
keep_scale = 1.0 / 0.9
sharpening_divisor = 0.05
epsilon = 1e-12

def bilinear_multiply(left, right):
    return jnp.einsum('...d,de->...e', left, right, precision=highest)

def layer_norm(row_block, gain_row, shift_row):
    row_mean = lax.optimization_barrier(jnp.mean(row_block, -1, keepdims=True))
    centred = row_block - row_mean
    variance = lax.optimization_barrier(jnp.mean(centred * centred, -1, keepdims=True))
    return centred * lax.rsqrt(variance + epsilon) * gain_row + shift_row

def one_block(weights, hidden, keep_one, keep_two, lens_group):
    query_w, key_w, value_w, output_w, inner_w, outer_w, pooler_w, query_b, value_b, output_b, gain_one, shift_one, inner_b, outer_b, gain_two, shift_two, pooler_b = weights
    group_count, length, model_width = hidden.shape
    head_count = model_width // HD
    head_scale = 1.0 / math.sqrt(HD)
    queries = low_back(low(bilinear_multiply(hidden, query_w) + query_b)).reshape(group_count, length, head_count, HD)
    key_rows = low_back(low(bilinear_multiply(hidden, key_w))).reshape(group_count, length, head_count, HD)
    value_rows = low_back(low(bilinear_multiply(hidden, value_w) + value_b)).reshape(group_count, length, head_count, HD)
    scores = jnp.einsum('gqhe,gkhe->ghqk', queries, key_rows, precision=highest) * head_scale
    key_valid = jnp.arange(length)[None, :] < lens_group[:, None]
    scores = low_back(jnp.where(key_valid[:, None, None, :], scores, -1000000000.0))
    prob_rows = low(jax.nn.softmax(scores, axis=-1))
    context = jnp.einsum('ghqk,gkhe->gqhe', prob_rows, value_rows, precision=highest)
    context = low_back(low(context.reshape(group_count, length, model_width)))
    attended = low_back(bilinear_multiply(context, output_w) + output_b)
    first_out = layer_norm(hidden[None] + attended[None] * keep_one * keep_scale, gain_one, shift_one)
    inner_pre = low_back(bilinear_multiply(low(first_out), inner_w) + inner_b)
    acted_rows = low(jax.nn.gelu(inner_pre, approximate=False))
    outer_out = low_back(bilinear_multiply(acted_rows, outer_w) + outer_b)
    second_out = layer_norm(first_out + outer_out * keep_two * keep_scale, gain_two, shift_two)
    pooled = low(second_out[:, :, 0, :])
    pre_act = low_back(bilinear_multiply(pooled, pooler_w) + pooler_b)
    tanh_out = jnp.tanh(pre_act)
    length_scaled_embeddings = low(tanh_out * lax.rsqrt(lax.optimization_barrier(jnp.sum(tanh_out * tanh_out, -1, keepdims=True)) + 1e-06))
    return (second_out, length_scaled_embeddings)

def whole_layer(weights, hidden, keep_one, keep_two, lengths):
    group_count = hidden.shape[0] // SENT_DEV
    stacked = (hidden.reshape(group_count, SENT_DEV, LEN, D), keep_one.reshape(2, group_count, SENT_DEV, LEN, D).transpose(1, 0, 2, 3, 4), keep_two.reshape(2, group_count, SENT_DEV, LEN, D).transpose(1, 0, 2, 3, 4), lengths.reshape(group_count, SENT_DEV))

    def apply_group(group_args):
        return one_block(weights, group_args[0], group_args[1], group_args[2], group_args[3])
    second_out, length_scaled_embeddings = lax.map(jax.checkpoint(apply_group), stacked)
    second_out = second_out.transpose(1, 0, 2, 3, 4).reshape(2, group_count * SENT_DEV, LEN, D)
    length_scaled_embeddings = length_scaled_embeddings.transpose(1, 0, 2, 3).reshape(2, group_count * SENT_DEV, D)
    cosine_scores = low_back(bilinear_multiply(length_scaled_embeddings[0], length_scaled_embeddings[1].T) / sharpening_divisor)
    loss_value = jnp.mean(jax.nn.logsumexp(cosine_scores, axis=-1) - jnp.diagonal(cosine_scores))
    return (second_out, loss_value)

def reference(hidden_in, attention_keep, feedforward_keep, lengths, cotangent, query_weight, key_weight, value_weight, output_weight, inner_weight, outer_weight, pooler_weight, query_bias, value_bias, output_bias, first_gain, first_shift, inner_bias, outer_bias, second_gain, second_shift, pooler_bias):
    weights = tuple((array.astype(jnp.float32) for array in (query_weight, key_weight, value_weight, output_weight, inner_weight, outer_weight, pooler_weight, query_bias, value_bias, output_bias, first_gain, first_shift, inner_bias, outer_bias, second_gain, second_shift, pooler_bias)))
    hidden = hidden_in.astype(jnp.float32)
    keep_one = attention_keep.astype(jnp.float32)
    keep_two = feedforward_keep.astype(jnp.float32)

    def forward(weight_set, hidden_rows):
        return whole_layer(weight_set, hidden_rows, keep_one, keep_two, lengths)
    (second_out, loss_value), pull_back = jax.vjp(forward, weights, hidden)
    weight_grads, hidden_grad = pull_back((cotangent.astype(jnp.float32), jnp.ones((), jnp.float32)))
    return (loss_value, second_out.astype(jnp.bfloat16), hidden_grad, weight_grads[0], weight_grads[1], weight_grads[2], weight_grads[3], weight_grads[4], weight_grads[5], weight_grads[6], weight_grads[7], weight_grads[8], weight_grads[9], weight_grads[10], weight_grads[11], weight_grads[12], weight_grads[13], weight_grads[14], weight_grads[15], weight_grads[16])
```

```python
import math

import jax
import jax.numpy as jnp
from jax import lax
from jax.sharding import PartitionSpec as P

HD = 64


keep_scale = 1.0 / 0.9
sharpening_divisor = 0.05
epsilon = 1e-12


def layer_norm(row_block, gain_row, shift_row):
    row_mean = jnp.mean(row_block, -1, keepdims=True)
    centred = row_block - row_mean
    variance = jnp.mean(centred * centred, -1, keepdims=True)
    return centred * lax.rsqrt(variance + epsilon) * gain_row + shift_row


def unit_vector(pre_act):
    tanh_out = jnp.tanh(pre_act)
    return tanh_out * lax.rsqrt(jnp.sum(tanh_out * tanh_out, -1, keepdims=True) + 1e-06)


def exact_gelu(inner_pre):
    return jax.nn.gelu(inner_pre, approximate=False)


def bilinear_multiply(left, right):
    return lax.dot_general(
        left, right, (((left.ndim - 1,), (0,)), ((), ())), preferred_element_type=jnp.float32
    )


def bilinear_multiply_flipped(left, right):
    return lax.dot_general(
        left, right, (((left.ndim - 1,), (1,)), ((), ())), preferred_element_type=jnp.float32
    )


def outer_sum(left, right):
    flat_left = left.reshape(-1, left.shape[-1])
    flat_right = right.reshape(-1, right.shape[-1])
    return lax.dot_general(
        flat_left, flat_right, (((0,), (0,)), ((), ())), preferred_element_type=jnp.float32
    )


def column_sum(rows_low):
    return jnp.sum(rows_low.astype(jnp.float32).reshape(-1, rows_low.shape[-1]), axis=0)


def attention_scores(queries, key_rows, key_valid):
    scores = jnp.einsum("gqhe,gkhe->ghqk", queries, key_rows, preferred_element_type=jnp.float32)
    scores = scores * (1.0 / math.sqrt(HD))
    return jnp.where(key_valid[:, None, None, :], scores, -1000000000.0)


def pack_shards(matrices, inner_weight, vectors, inner_bias):
    width = matrices[0].shape[1]
    row = jnp.concatenate(tuple(vectors) + (inner_bias,))
    row = jnp.pad(row[None, :], ((0, 7), (0, width - row.shape[0])))
    columns = [
        inner_weight[:, place : place + width] for place in range(0, inner_weight.shape[1], width)
    ]
    return jnp.concatenate(list(matrices) + columns + [row], axis=0)


def gather_doubling(block):
    count = lax.axis_size("dp")
    place = lax.axis_index("dp")
    bits = count.bit_length() - 1
    have = block[None]
    for bit in reversed(range(bits)):
        swap = [(source, source ^ (1 << bit)) for source in range(count)]
        other = lax.ppermute(have, "dp", swap)
        upper = ((place >> bit) & 1) == 1
        low_half = jnp.where(upper, other, have)
        high_half = jnp.where(upper, have, other)
        have = jnp.stack((low_half, high_half), axis=1).reshape((-1,) + block.shape)
    return have


def per_device(
    hidden_in,
    attention_keep,
    feedforward_keep,
    lengths,
    cotangent,
    query_weight,
    key_weight,
    value_weight,
    output_weight,
    inner_weight,
    outer_weight,
    pooler_weight,
    query_bias,
    value_bias,
    output_bias,
    first_gain,
    first_shift,
    inner_bias,
    outer_bias,
    second_gain,
    second_shift,
    pooler_bias,
):
    device_count = lax.axis_size("dp")
    packed = pack_shards(
        (query_weight, key_weight, value_weight, output_weight, outer_weight, pooler_weight),
        inner_weight,
        (
            query_bias,
            value_bias,
            output_bias,
            first_gain,
            first_shift,
            outer_bias,
            second_gain,
            second_shift,
            pooler_bias,
        ),
        inner_bias,
    )
    everyone = lax.all_gather(packed, "dp", axis=0, tiled=False)
    shard_rows = query_weight.shape[0]
    outer_rows = outer_weight.shape[0]
    full_width = hidden_in.shape[-1]
    starts = [0]
    for rows in (shard_rows,) * 4 + (outer_rows, shard_rows):
        starts.append(starts[-1] + rows)

    def whole(place, rows):
        return everyone[:, place : place + rows, :].reshape(device_count * rows, full_width)

    query_full = whole(starts[0], shard_rows)
    key_full = whole(starts[1], shard_rows)
    value_full = whole(starts[2], shard_rows)
    output_full = whole(starts[3], shard_rows)
    outer_full = whole(starts[4], outer_rows)
    pooler_full = whole(starts[5], shard_rows)
    inner_parts = inner_weight.shape[1] // full_width
    inner_full = jnp.concatenate(
        [whole(starts[6] + part * shard_rows, shard_rows) for part in range(inner_parts)], axis=1
    )
    vector_row = everyone[:, starts[6] + inner_parts * shard_rows, :]
    vectors = (
        vector_row[:, : 9 * shard_rows]
        .reshape(device_count, 9, shard_rows)
        .transpose(1, 0, 2)
        .reshape(9, full_width)
    )
    (
        query_bfull,
        value_bfull,
        output_bfull,
        gain_one,
        shift_one,
        outer_bfull,
        gain_two,
        shift_two,
        pooler_bfull,
    ) = [vectors[place] for place in range(9)]
    inner_bfull = vector_row[:, 9 * shard_rows : 9 * shard_rows + inner_bias.shape[0]].reshape(-1)
    sent_count, length, model_width = hidden_in.shape
    head_count = model_width // HD
    head_scale = 1.0 / math.sqrt(HD)
    key_valid = jnp.arange(length)[None, :] < lengths[:, None]
    queries = (
        (bilinear_multiply(hidden_in, query_full) + query_bfull)
        .astype(jnp.bfloat16)
        .reshape(sent_count, length, head_count, HD)
    )
    key_rows = (
        bilinear_multiply(hidden_in, key_full)
        .astype(jnp.bfloat16)
        .reshape(sent_count, length, head_count, HD)
    )
    value_rows = (
        (bilinear_multiply(hidden_in, value_full) + value_bfull)
        .astype(jnp.bfloat16)
        .reshape(sent_count, length, head_count, HD)
    )
    scores = attention_scores(queries, key_rows, key_valid)
    row_max = jnp.max(scores, -1, keepdims=True)
    log_total = row_max + jnp.log(jnp.sum(jnp.exp(scores - row_max), -1, keepdims=True))
    prob_low = jnp.exp(scores - log_total).astype(jnp.bfloat16)
    context = jnp.einsum(
        "ghqk,gkhe->gqhe", prob_low, value_rows, preferred_element_type=jnp.float32
    )
    context = context.reshape(sent_count, length, model_width).astype(jnp.bfloat16)
    attended = bilinear_multiply(context, output_full) + output_bfull
    keep_one = attention_keep.astype(jnp.float32)
    keep_two = feedforward_keep.astype(jnp.float32)
    first_in = hidden_in.astype(jnp.float32)[None] + attended[None] * keep_one * keep_scale
    first_out, first_pull = jax.vjp(
        layer_norm, first_in, gain_one.astype(jnp.float32), shift_one.astype(jnp.float32)
    )
    first_low = first_out.astype(jnp.bfloat16)
    inner_pre = bilinear_multiply(first_low, inner_full) + inner_bfull
    acted_rows, gelu_pull = jax.vjp(exact_gelu, inner_pre)
    acted_low = acted_rows.astype(jnp.bfloat16)
    outer_out = bilinear_multiply(acted_low, outer_full) + outer_bfull
    second_in = first_out + outer_out * keep_two * keep_scale
    second_out, second_pull = jax.vjp(
        layer_norm, second_in, gain_two.astype(jnp.float32), shift_two.astype(jnp.float32)
    )
    hidden_out = second_out.astype(jnp.bfloat16)
    pooled = second_out[:, :, 0, :].astype(jnp.bfloat16)
    pre_act = bilinear_multiply(pooled, pooler_full) + pooler_bfull
    length_scaled_embeddings, unit_pull = jax.vjp(unit_vector, pre_act)
    sphere_summed_embeddings = length_scaled_embeddings.astype(jnp.bfloat16)
    both_views = gather_doubling(sphere_summed_embeddings)
    firsts = both_views[:, 0].reshape(-1, model_width)
    contrast_examples = both_views[:, 1].reshape(-1, model_width)
    cosine_scores = bilinear_multiply_flipped(firsts, contrast_examples) / sharpening_divisor
    total_rows = contrast_examples.shape[0]
    is_target = jnp.arange(total_rows)[None, :] == jnp.arange(total_rows)[:, None]
    logit_max = jnp.max(cosine_scores, -1, keepdims=True)
    log_sums = logit_max + jnp.log(jnp.sum(jnp.exp(cosine_scores - logit_max), -1, keepdims=True))
    picked = jnp.sum(jnp.where(is_target, cosine_scores, 0.0), -1)
    loss_value = jnp.sum(log_sums[:, 0] - picked) / total_rows
    row_share = 1.0 / total_rows
    softmax_rows = jnp.exp(cosine_scores - log_sums)
    cosine_score_derivative = (
        softmax_rows * row_share - jnp.where(is_target, row_share, 0.0)
    ).astype(jnp.bfloat16)
    own_start = lax.axis_index("dp") * sent_count
    own_rows = lax.dynamic_slice_in_dim(cosine_score_derivative, own_start, sent_count, 0)
    own_columns = lax.dynamic_slice_in_dim(cosine_score_derivative, own_start, sent_count, 1)
    matched_view_derivative = (
        bilinear_multiply(own_rows, contrast_examples) / sharpening_divisor
    )
    far_grad = (
        lax.dot_general(
            own_columns, firsts, (((0,), (0,)), ((), ())), preferred_element_type=jnp.float32
        )
        / sharpening_divisor
    )
    query_back, key_back, value_back, output_back, inner_back, outer_back, pooler_back = (
        query_full,
        key_full,
        value_full,
        output_full,
        inner_full,
        outer_full,
        pooler_full,
    )
    (pre_grad,) = unit_pull(jnp.stack([matched_view_derivative, far_grad]))
    pre_low = pre_grad.astype(jnp.bfloat16)
    pooler_wgrad = outer_sum(pooled, pre_low)
    pooler_bgrad = column_sum(pre_low)
    pooled_back = bilinear_multiply_flipped(pre_low, pooler_back)
    out_grad = cotangent.astype(jnp.float32).at[:, :, 0, :].add(pooled_back)
    second_grad, gain_two_grad, shift_two_grad = second_pull(out_grad)
    outer_low = (second_grad * keep_two * keep_scale).astype(jnp.bfloat16)
    outer_wgrad = outer_sum(acted_low, outer_low)
    outer_bgrad = column_sum(outer_low)
    (inner_grad,) = gelu_pull(bilinear_multiply_flipped(outer_low, outer_back))
    inner_low = inner_grad.astype(jnp.bfloat16)
    inner_wgrad = outer_sum(first_low, inner_low)
    inner_bgrad = column_sum(inner_low)
    first_grad = second_grad + bilinear_multiply_flipped(inner_low, inner_back)
    in_grad, gain_one_grad, shift_one_grad = first_pull(first_grad)
    attended_low = jnp.sum(in_grad * keep_one * keep_scale, axis=0).astype(jnp.bfloat16)
    output_wgrad = outer_sum(context, attended_low)
    output_bgrad = column_sum(attended_low)
    context_grad = (
        bilinear_multiply_flipped(attended_low, output_back)
        .astype(jnp.bfloat16)
        .reshape(sent_count, length, head_count, HD)
    )
    again_scores = attention_scores(queries, key_rows, key_valid)
    prob_rows = jnp.exp(again_scores - log_total)
    prob_again = prob_rows.astype(jnp.bfloat16)
    value_grad = jnp.einsum(
        "ghqk,gqhe->gkhe", prob_again, context_grad, preferred_element_type=jnp.float32
    )
    prob_grad = jnp.einsum(
        "gqhe,gkhe->ghqk", context_grad, value_rows, preferred_element_type=jnp.float32
    )
    score_low = (
        prob_rows * (prob_grad - jnp.sum(prob_rows * prob_grad, -1, keepdims=True))
    ).astype(jnp.bfloat16)
    query_grad = (
        jnp.einsum("ghqk,gkhe->gqhe", score_low, key_rows, preferred_element_type=jnp.float32)
        * head_scale
    )
    key_grad = (
        jnp.einsum("ghqk,gqhe->gkhe", score_low, queries, preferred_element_type=jnp.float32)
        * head_scale
    )
    query_low = query_grad.astype(jnp.bfloat16).reshape(sent_count, length, model_width)
    key_low = key_grad.astype(jnp.bfloat16).reshape(sent_count, length, model_width)
    value_low = value_grad.astype(jnp.bfloat16).reshape(sent_count, length, model_width)
    query_wgrad = outer_sum(hidden_in, query_low)
    query_bgrad = column_sum(query_low)
    key_wgrad = outer_sum(hidden_in, key_low)
    value_wgrad = outer_sum(hidden_in, value_low)
    value_bgrad = column_sum(value_low)
    hidden_grad = (
        jnp.sum(in_grad, axis=0)
        + bilinear_multiply_flipped(query_low, query_back)
        + bilinear_multiply_flipped(key_low, key_back)
        + bilinear_multiply_flipped(value_low, value_back)
    )
    low = jnp.bfloat16

    def split_rows(grad):
        return grad.astype(low).reshape(device_count, -1, full_width)

    vector_grads = jnp.stack(
        (
            query_bgrad,
            value_bgrad,
            output_bgrad,
            gain_one_grad,
            shift_one_grad,
            outer_bgrad,
            gain_two_grad,
            shift_two_grad,
            pooler_bgrad,
        )
    )
    vector_part = (
        vector_grads.reshape(9, device_count, shard_rows)
        .transpose(1, 0, 2)
        .reshape(device_count, 9 * shard_rows)
    )
    vector_part = jnp.concatenate((vector_part, inner_bgrad.reshape(device_count, -1)), axis=1)
    vector_part = jnp.pad(
        vector_part.astype(low)[:, None, :],
        ((0, 0), (0, 7), (0, full_width - vector_part.shape[1])),
    )
    grads = jnp.concatenate(
        [
            split_rows(query_wgrad),
            split_rows(key_wgrad),
            split_rows(value_wgrad),
            split_rows(output_wgrad),
            split_rows(outer_wgrad),
            split_rows(pooler_wgrad),
        ]
        + [
            split_rows(inner_wgrad[:, part * full_width : (part + 1) * full_width])
            for part in range(inner_parts)
        ]
        + [vector_part],
        axis=1,
    )
    packed_rows = grads.shape[1]
    sums = lax.psum_scatter(
        grads.reshape(device_count * packed_rows, full_width), "dp", scatter_dimension=0, tiled=True
    ).astype(jnp.float32)
    query_sum = sums[starts[0] : starts[1]]
    key_sum = sums[starts[1] : starts[2]]
    value_sum = sums[starts[2] : starts[3]]
    output_sum = sums[starts[3] : starts[4]]
    outer_sum_w = sums[starts[4] : starts[5]]
    pooler_sum = sums[starts[5] : starts[6]]
    inner_sum_w = jnp.concatenate(
        [
            sums[starts[6] + part * shard_rows : starts[6] + (part + 1) * shard_rows]
            for part in range(inner_parts)
        ],
        axis=1,
    )
    vector_sum = sums[starts[6] + inner_parts * shard_rows]
    (
        query_bsum,
        value_bsum,
        output_bsum,
        gain_one_sum,
        shift_one_sum,
        outer_bsum,
        gain_two_sum,
        shift_two_sum,
        pooler_bsum,
    ) = [vector_sum[place * shard_rows : (place + 1) * shard_rows] for place in range(9)]
    inner_bsum = vector_sum[9 * shard_rows : 9 * shard_rows + inner_bias.shape[0]]
    return (
        loss_value,
        hidden_out,
        hidden_grad,
        query_sum,
        key_sum,
        value_sum,
        output_sum,
        inner_sum_w,
        outer_sum_w,
        pooler_sum,
        query_bsum,
        value_bsum,
        output_bsum,
        gain_one_sum,
        shift_one_sum,
        inner_bsum,
        outer_bsum,
        gain_two_sum,
        shift_two_sum,
        pooler_bsum,
    )


def solution(mesh):
    in_specs = (
        P("dp", None, None),
        P(None, "dp", None, None),
        P(None, "dp", None, None),
        P("dp"),
        P(None, "dp", None, None),
        P("dp", None),
        P("dp", None),
        P("dp", None),
        P("dp", None),
        P("dp", None),
        P("dp", None),
        P("dp", None),
        P("dp"),
        P("dp"),
        P("dp"),
        P("dp"),
        P("dp"),
        P("dp"),
        P("dp"),
        P("dp"),
        P("dp"),
        P("dp"),
    )
    out_specs = (
        P(),
        P(None, "dp", None, None),
        P("dp", None, None),
        P("dp", None),
        P("dp", None),
        P("dp", None),
        P("dp", None),
        P("dp", None),
        P("dp", None),
        P("dp", None),
        P("dp"),
        P("dp"),
        P("dp"),
        P("dp"),
        P("dp"),
        P("dp"),
        P("dp"),
        P("dp"),
        P("dp"),
        P("dp"),
    )
    return jax.shard_map(
        per_device, mesh=mesh, in_specs=in_specs, out_specs=out_specs, check_vma=False
    )
```
